32 devices in a mesh: seq: 4 (over y, core), vocab: 8 (over z, x).
Axes of the slice: x: 2, y: 2, z: 4, core: 2. Of those that a mesh axis runs over, the one named last changes fastest.
Arguments:
- hidden: bfloat16 [2, 512, 5120], P(None, 'seq'), may hold values from -128 to 128
- head_weight: bfloat16 [5120, 77824], P('seq', 'vocab'), may hold values from -1 to 1
- ref_logits: bfloat16 [2, 512, 77824], P(None, 'seq', 'vocab'), may hold values from -320 to 320
- token_ids: int32 [2, 512], P(None, 'seq'), may hold values from 0 to 77823
- end_pos: int32 [2], replicated, may hold values from 256 to 511
- loss_mask: int32 [2, 512], P(None, 'seq'), may hold values 0 or 1
- scores: float32 [2], replicated, may hold values from -8 to 8
Outputs:
- logit_grad: bfloat16 [2, 512, 77824], P(None, 'seq', 'vocab')
- hidden_grad: bfloat16 [2, 512, 5120], P(None, 'seq', 'vocab')
- advantages: float32 [2, 512], P(None, 'seq')
The draws below stay inside these ranges and needn't reach their ends.
All inputs are finite; a program needn't handle non-finite values. No bound on the sum of `loss_mask` on one device may be relied on, other than what follows from the above.
Results may differ from the reference program's by a relative error of at most 0.0039.
The reference program's roundings to bfloat16 on the way count: a program that leaves them out, or rounds other values in their place, can miss the bound.
Values may be sent and summed in bfloat16 or wider, within the bound.
A program may use at most 128 MiB of HBM per device.

```python
import math
import jax
import jax.numpy as jnp
from jax import lax

D = 5120
VOCAB = 77824
BATCH = 2
SEQ_LEN = 512


HIDDEN_LIMIT = 128.0


def special_columns(key):
    base = jax.random.fold_in(key, 77)
    keys = jax.random.split(base, 4)
    first_index = jax.random.randint(keys[0], (), 0, VOCAB)
    second_index = (first_index + 1 + jax.random.randint(keys[1], (), 0, VOCAB - 1)) % VOCAB
    first_col = jax.random.normal(keys[2], (D,), jnp.float32) / math.sqrt(D)
    second_col = jax.random.normal(keys[3], (D,), jnp.float32) / math.sqrt(D)
    second_col = second_col - jnp.dot(second_col, first_col) / jnp.dot(first_col, first_col) * first_col
    return (first_index, second_index, first_col, second_col)


def head_column(key, column_index, specials):
    first_index, second_index, first_col, second_col = specials
    column = jax.random.normal(jax.random.fold_in(jax.random.fold_in(key, 5), column_index), (D,), jnp.float32)
    column = jnp.clip(column, -6.0, 6.0) / math.sqrt(D)
    column = jnp.where(column_index == first_index, first_col, column)
    return jnp.where(column_index == second_index, second_col, column)


def token_draw(key):
    return jax.random.randint(jax.random.fold_in(key, 31), (BATCH, SEQ_LEN), 0, VOCAB).astype(jnp.int32)


def draw_token_ids(key, part):
    return token_draw(key)


def draw_head_weight(key, part):
    specials = special_columns(key)
    columns = jax.vmap(lambda column_index: head_column(key, column_index, specials))(jnp.arange(VOCAB).astype(jnp.int32))
    return jnp.transpose(columns).astype(jnp.bfloat16)


def draw_hidden(key, part):
    states = 3.0 * jnp.clip(jax.random.normal(jax.random.fold_in(key, 6), (BATCH, SEQ_LEN, D), jnp.float32), -6.0, 6.0)
    specials = special_columns(key)
    tokens = token_draw(key).reshape(BATCH * SEQ_LEN)
    token_columns = jax.vmap(lambda column_index: head_column(key, column_index, specials))(tokens)
    token_columns = token_columns.reshape(BATCH, SEQ_LEN, D)
    boost_size = jax.random.uniform(jax.random.fold_in(key, 10), (BATCH, SEQ_LEN, 1), jnp.float32, 6.0, 19.0)
    states = states + boost_size * token_columns / jnp.sum(token_columns * token_columns, axis=2, keepdims=True)
    states = jnp.clip(states, -HIDDEN_LIMIT, HIDDEN_LIMIT)
    return states.astype(jnp.bfloat16)


def draw_ref_logits(key, part):
    values = 1.5 * jnp.clip(jax.random.normal(jax.random.fold_in(key, 21), (BATCH, SEQ_LEN, VOCAB), jnp.float32), -6.0, 6.0)
    return values.astype(jnp.bfloat16)


def with_ends(values, stream_key, low, top_value):
    shape = values.shape
    spot = [jax.random.randint(jax.random.fold_in(stream_key, axis), (), 0, shape[axis]) for axis in range(len(shape))]
    values = values.at[tuple(spot)].set(low)
    longest = shape.index(max(shape))
    spot[longest] = (spot[longest] + 1) % shape[longest]
    return values.at[tuple(spot)].set(top_value)


def centred(own_key, extent, scale, bound, held_as=jnp.bfloat16):
    result = scale * jax.random.normal(own_key, extent, jnp.float32)
    return jnp.clip(result, min=-bound, max=bound).astype(held_as)


def setup_inputs(seed: int = 0) -> dict:
    splits = jax.random.split(jax.random.key(seed), 8)
    return {
        "hidden": draw_hidden(jax.random.fold_in(splits[7], 71), 0),
        "head_weight": draw_head_weight(jax.random.fold_in(splits[7], 71), 0),
        "ref_logits": draw_ref_logits(jax.random.fold_in(splits[7], 71), 0),
        "token_ids": draw_token_ids(jax.random.fold_in(splits[7], 71), 0),
        "end_pos": jax.random.randint(splits[4], (BATCH,), SEQ_LEN // 2, SEQ_LEN).astype(jnp.int32),
        "loss_mask": with_ends((jax.random.randint(splits[5], (BATCH, SEQ_LEN), 0, 4) < 3).astype(jnp.int32), jax.random.fold_in(splits[5], 1), 0, 1),
        "scores": centred(splits[6], (BATCH,), 2.0, 8.0, jnp.float32),
    }


def row_stats(pair, head_weight):
    states, refs = pair
    logits = jnp.dot(states, head_weight, preferred_element_type=jnp.float32)
    refs = refs.astype(jnp.float32)
    top_policy = lax.optimization_barrier(jnp.max(logits, axis=1))
    expo = jnp.exp(logits - top_policy[:, None])
    total = lax.optimization_barrier(jnp.sum(expo, axis=1))
    weighted = lax.optimization_barrier(jnp.sum(expo * (logits - refs), axis=1))
    top_ref = lax.optimization_barrier(jnp.max(refs, axis=1))
    ref_total = lax.optimization_barrier(jnp.sum(jnp.exp(refs - top_ref[:, None]), axis=1))
    lse_policy = top_policy + jnp.log(total)
    lse_ref = top_ref + jnp.log(ref_total)
    return weighted / total - lse_policy + lse_ref

def grad_rows(triple, head_weight):
    states, tokens, factor = triple
    logits = jnp.dot(states, head_weight, preferred_element_type=jnp.float32)
    top_policy = lax.optimization_barrier(jnp.max(logits, axis=1))
    lse_policy = top_policy + jnp.log(lax.optimization_barrier(jnp.sum(jnp.exp(logits - top_policy[:, None]), axis=1)))
    prob = jnp.exp(logits - lse_policy[:, None])
    column = jnp.arange(logits.shape[1]).astype(jnp.int32)
    onehot = (column[None, :] == tokens[:, None]).astype(jnp.float32)
    grad = (factor[:, None] * (prob - onehot)).astype(jnp.bfloat16)
    back = jnp.dot(grad, head_weight.T, preferred_element_type=jnp.float32).astype(jnp.bfloat16)
    return (grad, back)

def reference(hidden, head_weight, ref_logits, token_ids, end_pos, loss_mask, scores):
    kl_value = lax.map(lambda pair: row_stats(pair, head_weight), (hidden, ref_logits))
    position = jnp.arange(SEQ_LEN).astype(jnp.int32)
    live = ((loss_mask == 1) & (position[None, :] <= end_pos[:, None])).astype(jnp.float32)
    at_end = (position[None, :] == end_pos[:, None]).astype(jnp.float32)
    reward = -0.01 * kl_value * live + scores[:, None] * at_end
    returns = jnp.cumsum(reward[:, ::-1], axis=1)[:, ::-1]
    count = jnp.maximum(jnp.sum(live), 1.0)
    mean = jnp.sum(live * returns) / count
    var = jnp.sum(live * returns * returns) / count - mean * mean
    advantages = (returns - mean) / jnp.sqrt(var + 1e-05)
    factor = live * advantages / count
    logit_grad, hidden_grad = lax.map(lambda triple: grad_rows(triple, head_weight), (hidden, token_ids, factor))
    return (logit_grad, hidden_grad, advantages)
```

```python
import functools

import jax
import jax.numpy as jnp
from jax import lax
from jax.experimental import pallas as pl
from jax.experimental.pallas import tpu as pltpu
from jax.sharding import PartitionSpec as P


CORES = 2
FORWARD_CHUNKS = 8
EARLY_CHUNKS = 2
LEVELS = 32767.0


def pieces(extent, parts, unit=128):
    blocks = extent // unit
    edges = [unit * (blocks * i // parts) for i in range(parts)] + [extent]
    return [(lo, hi) for lo, hi in zip(edges[:-1], edges[1:]) if hi > lo]


def exchange_kernel(axis, n, x_ref, out_ref, send_sem, recv_sem, local_sem):
    me = lax.axis_index(axis)
    barrier = pltpu.get_barrier_semaphore()
    for k in range(1, n):
        pl.semaphore_signal(
            barrier,
            inc=1,
            device_id={axis: lax.rem(me + k, n)},
            device_id_type=pl.DeviceIdType.MESH,
        )
    own = pltpu.make_async_copy(x_ref, out_ref.at[me], local_sem)
    own.start()
    pl.semaphore_wait(barrier, n - 1)
    copies = []
    for k in range(1, n):
        copy = pltpu.make_async_remote_copy(
            src_ref=x_ref,
            dst_ref=out_ref.at[me],
            send_sem=send_sem.at[k],
            recv_sem=recv_sem.at[k],
            device_id={axis: lax.rem(me + k, n)},
            device_id_type=pl.DeviceIdType.MESH,
        )
        copy.start()
        copies.append(copy)
    own.wait()
    for copy in copies:
        copy.wait()


def exchange(x, axis, collective_id):
    n = lax.axis_size(axis)
    return pl.pallas_call(
        functools.partial(exchange_kernel, axis, n),
        out_shape=jax.ShapeDtypeStruct((n,) + x.shape, x.dtype),
        in_specs=[pl.BlockSpec(memory_space=pltpu.VMEM)],
        out_specs=pl.BlockSpec(memory_space=pltpu.VMEM),
        scratch_shapes=[
            pltpu.SemaphoreType.DMA((n,)),
            pltpu.SemaphoreType.DMA((n,)),
            pltpu.SemaphoreType.DMA,
        ],
        compiler_params=pltpu.CompilerParams(
            collective_id=collective_id, has_side_effects=True
        ),
    )(x)


def rows_of(stack, rows):
    flat = jnp.concatenate(stack, axis=0)
    return jnp.pad(flat, ((0, rows - flat.shape[0]), (0, 0)))


def compute(hidden, head_weight, ref_logits, token_ids, end_pos, loss_mask, scores):
    batch, segment, width = hidden.shape
    rows, vocab_dev = head_weight.shape
    seq_size = lax.axis_size("seq")
    vocab_size = lax.axis_size("vocab")
    chips = seq_size // CORES
    seq = lax.axis_index("seq")
    vocab = lax.axis_index("vocab")
    chip, core = seq // CORES, seq % CORES
    vocab_start = vocab * vocab_dev

    def sibling(x):
        return lax.ppermute(x, "seq", [(s, s ^ 1) for s in range(seq_size)])

    def shift(x, by):
        pairs = [(s, (s + CORES * by) % seq_size) for s in range(seq_size)]
        return lax.ppermute(x, "seq", pairs)

    def features(owner):
        mine = lax.dynamic_slice_in_dim(hidden, owner * rows, rows, axis=2)
        other = lax.dynamic_slice_in_dim(hidden, (owner ^ 1) * rows, rows, axis=2)
        return jnp.concatenate([mine, other], axis=2)

    chunks = pieces(vocab_dev, FORWARD_CHUNKS)
    outgoing = [features((seq - CORES * r) % seq_size) for r in range(1, chips)]
    own_states = features(seq)
    arriving = [shift(x, -r) for r, x in enumerate(outgoing, 1)]
    swapped = lax.optimization_barrier((head_weight, *outgoing))[0]
    weights = [(head_weight[:, lo:hi], sibling(swapped[:, lo:hi])) for lo, hi in chunks]

    def project(x, pair):
        mine, other = pair
        dot = functools.partial(
            jnp.einsum, "nbsd,dv->nbsv", preferred_element_type=jnp.float32
        )
        return dot(x[..., :rows], mine) + dot(x[..., rows:], other)

    def encode(x):
        top = jnp.maximum(jnp.max(jnp.abs(x), axis=-1), 1e-30)
        code = jnp.round(x * (LEVELS / top)[..., None]).astype(jnp.int16)
        return code, top / LEVELS

    def decode(code, step):
        return code.astype(jnp.float32) * step[..., None]

    states = jnp.stack([*arriving, own_states])
    logits, tops, totals, weighteds = [], [], [], []
    partials, sent = [], []
    for pair in weights:
        part = project(states, pair)
        partials.append(part[chips - 1])
        hops = []
        for r in range(1, chips):
            code, step = encode(part[r - 1])
            hops.append((shift(code, r), shift(step, r)))
        sent.append(hops)
    for j, (lo, hi) in enumerate(chunks):
        part = partials[j]
        for code, step in sent[j]:
            part = part + decode(code, step)
        logits.append(part)
        top = jnp.max(part, axis=2)
        expo = jnp.exp(part - top[:, :, None])
        refs = ref_logits[:, :, lo:hi].astype(jnp.float32)
        tops.append(top)
        totals.append(jnp.sum(expo, axis=2))
        weighteds.append(jnp.sum(expo * (part - refs), axis=2))
    refs = ref_logits.astype(jnp.float32)
    local_rtop = jnp.max(refs, axis=2)
    local_rtotal = jnp.sum(jnp.exp(refs - local_rtop[:, :, None]), axis=2)
    early = []
    for part in logits[:EARLY_CHUNKS]:
        code, step = encode(part)
        early.append([(shift(code, -r), shift(step, -r)) for r in range(1, chips)])

    def merge(top_list, sums_list):
        top = functools.reduce(jnp.maximum, top_list)
        scales = [jnp.exp(t - top) for t in top_list]
        return top, [
            functools.reduce(jnp.add, [s * x for s, x in zip(scales, sums)])
            for sums in sums_list
        ]

    local_top, (local_total, local_weighted) = merge(tops, (totals, weighteds))
    stats = exchange(
        rows_of((local_top, local_total, local_weighted, local_rtop, local_rtotal), 16),
        "vocab",
        0,
    )
    stats = [
        [stats[d, batch * i : batch * (i + 1)] for d in range(vocab_size)] for i in range(5)
    ]
    top_policy, (total, weighted) = merge(stats[0], (stats[1], stats[2]))
    top_ref, (ref_total,) = merge(stats[3], (stats[4],))
    lse_policy = top_policy + jnp.log(total)
    lse_ref = top_ref + jnp.log(ref_total)
    kl_value = weighted / total - lse_policy + lse_ref
    position = seq * segment + lax.broadcasted_iota(jnp.int32, (1, segment), 1)
    live = ((loss_mask == 1) & (position <= end_pos[:, None])).astype(jnp.float32)
    at_end = (position == end_pos[:, None]).astype(jnp.float32)
    reward = -0.01 * kl_value * live + scores[:, None] * at_end
    table = rows_of((reward, live, lse_policy, token_ids.astype(jnp.float32)), 4 * batch)
    everyone = exchange(table, "seq", 1)
    all_reward, all_live, all_lse, all_tokens = [
        everyone[:, batch * i : batch * (i + 1)] for i in range(4)
    ]
    upper = (
        lax.broadcasted_iota(jnp.int32, (segment, segment), 0)
        >= lax.broadcasted_iota(jnp.int32, (segment, segment), 1)
    ).astype(jnp.float32)
    returns = jnp.einsum("nbs,st->nbt", all_reward, upper, precision=lax.Precision.HIGHEST)
    block_totals = jnp.sum(all_reward, axis=2)
    carried = [jnp.zeros_like(block_totals[0])]
    for s in range(seq_size - 1, 0, -1):
        carried.append(carried[-1] + block_totals[s])
    returns = returns + jnp.stack(carried[::-1])[:, :, None]
    count = jnp.maximum(jnp.sum(all_live), 1.0)
    mean = jnp.sum(all_live * returns) / count
    var = jnp.sum(all_live * returns * returns) / count - mean * mean
    all_advantages = (returns - mean) / jnp.sqrt(var + 1e-05)
    all_factor = all_live * all_advantages / count

    def of(x, owner):
        return lax.dynamic_index_in_dim(x, owner, 0, keepdims=False)

    def gradient(part, lo, hi, owner, tokens, lse):
        prob = jnp.exp(part - lse[:, :, None])
        column = vocab_start + lo + lax.broadcasted_iota(jnp.int32, (1, 1, hi - lo), 2)
        onehot = (column == tokens[:, :, None]).astype(jnp.float32)
        return (of(all_factor, owner)[:, :, None] * (prob - onehot)).astype(jnp.bfloat16)

    advantages = of(all_advantages, seq)
    grads = [
        gradient(part, lo, hi, seq, token_ids, lse_policy)
        for (lo, hi), part in zip(chunks, logits)
    ]
    logit_grad = jnp.concatenate(grads, axis=2)

    blocks = vocab_size // chips
    block = width // vocab_size
    part_rows = block // chips

    def back(terms):
        halves = []
        for g, pair in terms:
            g = lax.optimization_barrier((g, *halves))[0]
            dots = [
                jnp.einsum("dv,tv->dt", w, g, preferred_element_type=jnp.float32)
                for w in pair
            ]
            halves = [h + d for h, d in zip(halves, dots)] if halves else dots
        return halves

    low_bits = [1 << i for i in range((vocab_size // CORES).bit_length() - 1)]
    top_bit = vocab_size // CORES

    def reduce_vocab(halves, turn):
        rest = jnp.concatenate(halves, axis=0)
        tokens = rest.shape[1]
        bits = low_bits[turn:] + low_bits[:turn]
        lengths = [2] * (len(low_bits) + 1)
        rest = rest.reshape(*lengths, part_rows, tokens)
        left = [top_bit] + low_bits[::-1]
        for bit in bits + [top_bit]:
            axis = left.index(bit)
            left.remove(bit)
            mine = (vocab // bit) % 2
            if bit == top_bit:
                mine = mine ^ core
            keep = lax.dynamic_index_in_dim(rest, mine, axis, keepdims=False)
            give = lax.dynamic_index_in_dim(rest, 1 - mine, axis, keepdims=False)
            rest = keep + lax.ppermute(
                give, "vocab", [(v, v ^ bit) for v in range(vocab_size)]
            )
        return rest

    def reduce_all(halves):
        return [
            reduce_vocab([h[:, b * segment : (b + 1) * segment] for h in halves], b % 2)
            for b in range(batch)
        ]

    flat = [x.reshape(batch * segment, -1) for x in grads]
    late = [[shift(g, -r) for r in range(1, chips)] for g in flat[EARLY_CHUNKS:]]
    received = []
    for r in range(1, chips):
        owner = (seq + CORES * r) % seq_size
        tokens = of(all_tokens, owner).astype(jnp.int32)
        lse = of(all_lse, owner)
        first = [
            gradient(decode(*hops[r - 1]), lo, hi, owner, tokens, lse).reshape(batch * segment, -1)
            for (lo, hi), hops in zip(chunks, early)
        ]
        received.append(first + [hops[r - 1] for hops in late])

    latest = back(zip(lax.optimization_barrier(flat), weights))
    owned = [reduce_all(latest)]
    for arrived in received:
        arrived = [lax.optimization_barrier((g, *latest))[0] for g in arrived]
        latest = back(zip(arrived, weights))
        owned.append(reduce_all(latest))
    held = jnp.stack([jnp.stack(parts, axis=1) for parts in owned]).astype(jnp.bfloat16)

    mine_q = vocab % chips
    source = vocab // blocks
    hidden_grad = jnp.zeros((chips, part_rows, batch, segment), jnp.bfloat16)
    for k in range(chips):
        pairs = []
        for s in range(seq_size):
            for v in range(vocab_size):
                y, c = divmod(s, CORES)
                to = ((y + k - v % chips) % chips) * CORES + c
                pairs.append((s * vocab_size + v, to * vocab_size + blocks * y + v // chips))
        out = lax.dynamic_index_in_dim(held, (k - mine_q) % chips, 0, keepdims=False)
        got = lax.ppermute(out, ("seq", "vocab"), pairs)
        hidden_grad = lax.dynamic_update_index_in_dim(
            hidden_grad, got, (k - (chip - source)) % chips, 0
        )
    hidden_grad = jnp.transpose(hidden_grad.reshape(block, batch, segment), (1, 2, 0))
    return (logit_grad, hidden_grad, advantages)


def solution(mesh):
    in_specs = (
        P(None, "seq", None),
        P("seq", "vocab"),
        P(None, "seq", "vocab"),
        P(None, "seq"),
        P(),
        P(None, "seq"),
        P(),
    )
    out_specs = (P(None, "seq", "vocab"), P(None, "seq", "vocab"), P(None, "seq"))
    return jax.shard_map(
        compute, mesh=mesh, in_specs=in_specs, out_specs=out_specs, check_vma=False
    )
```

```python
import functools

import jax
import jax.numpy as jnp
from jax import lax
from jax.experimental import pallas as pl
from jax.experimental.pallas import tpu as pltpu
from jax.sharding import PartitionSpec as P


CORES = 2
FORWARD_CHUNKS = 8
EARLY_CHUNKS = 3
LAST_CHUNKS = 2
LANES = 128
RING = 256 * 9728
SLOTS = 3
LEVELS = 32767.0


def pieces(extent, parts, unit=128):
    blocks = extent // unit
    edges = [unit * (blocks * i // parts) for i in range(parts)] + [extent]
    return [(lo, hi) for lo, hi in zip(edges[:-1], edges[1:]) if hi > lo]


def exchange_kernel(axis, n, x_ref, out_ref, send_sem, recv_sem, local_sem):
    me = lax.axis_index(axis)
    barrier = pltpu.get_barrier_semaphore()
    for k in range(1, n):
        pl.semaphore_signal(
            barrier,
            inc=1,
            device_id={axis: lax.rem(me + k, n)},
            device_id_type=pl.DeviceIdType.MESH,
        )
    own = pltpu.make_async_copy(x_ref, out_ref.at[me], local_sem)
    own.start()
    pl.semaphore_wait(barrier, n - 1)
    copies = []
    for k in range(1, n):
        copy = pltpu.make_async_remote_copy(
            src_ref=x_ref,
            dst_ref=out_ref.at[me],
            send_sem=send_sem.at[k],
            recv_sem=recv_sem.at[k],
            device_id={axis: lax.rem(me + k, n)},
            device_id_type=pl.DeviceIdType.MESH,
        )
        copy.start()
        copies.append(copy)
    own.wait()
    for copy in copies:
        copy.wait()


def exchange(x, axis, collective_id):
    n = lax.axis_size(axis)
    return pl.pallas_call(
        functools.partial(exchange_kernel, axis, n),
        out_shape=jax.ShapeDtypeStruct((n,) + x.shape, x.dtype),
        in_specs=[pl.BlockSpec(memory_space=pltpu.VMEM)],
        out_specs=pl.BlockSpec(memory_space=pltpu.VMEM),
        scratch_shapes=[
            pltpu.SemaphoreType.DMA((n,)),
            pltpu.SemaphoreType.DMA((n,)),
            pltpu.SemaphoreType.DMA,
        ],
        compiler_params=pltpu.CompilerParams(
            collective_id=collective_id, has_side_effects=True
        ),
    )(x)


def back_kernel(steps, depth, lo, widths, has_base, *refs):
    mine_ref, other_ref = refs[:2]
    grads = refs[2 : 2 + len(widths)]
    base = refs[2 + len(widths)] if has_base else None
    out_ref, ring, sems = refs[-3:]
    slots = ring.shape[0]
    step = pl.program_id(0)

    def copy(w_ref, row, slot):
        rows = pl.ds(pl.multiple_of(row * depth, depth), depth)
        return pltpu.make_async_copy(
            w_ref.at[rows, lo : lo + sum(widths)], ring.at[slot], sems.at[slot]
        )

    def fetch(item):
        slot = lax.rem(item, slots)
        pl.when(item < steps)(lambda: copy(mine_ref, item, slot).start())
        pl.when((item >= steps) & (item < 2 * steps))(
            lambda: copy(other_ref, item - steps, slot).start()
        )

    @pl.when(step == 0)
    def _():
        for item in range(slots - 1):
            fetch(jnp.int32(item))

    fetch(step + slots - 1)
    slot = lax.rem(step, slots)
    copy(mine_ref, 0, slot).wait()
    total = None
    start = 0
    for grad, width in zip(grads, widths):
        term = lax.dot_general(
            ring[slot, :, start : start + width],
            grad[...],
            (((1,), (1,)), ((), ())),
            preferred_element_type=jnp.float32,
        )
        total = term if total is None else total + term
        start += width
    out_ref[...] = total if base is None else total + base[...]


def back(mine, other, lo, grads, base=None):
    rows = mine.shape[0]
    tokens = grads[0].shape[0]
    widths = [g.shape[1] for g in grads]
    width = sum(widths)
    fits = [rows // n for n in range(1, rows // 16 + 1) if rows % (16 * n) == 0]
    depth = next((d for d in fits if d * width <= RING), 16)
    steps = rows // depth
    specs = [pl.BlockSpec(memory_space=pl.ANY)] * 2
    specs += [
        pl.BlockSpec((tokens, w), lambda i: (0, 0), pipeline_mode=pl.Buffered(1)) for w in widths
    ]
    operands = [mine, other, *grads]
    if base is not None:
        specs.append(pl.BlockSpec((depth, tokens), lambda i: (i, 0)))
        operands.append(base)
    return pl.pallas_call(
        functools.partial(back_kernel, steps, depth, lo, widths, base is not None),
        grid=(2 * steps,),
        out_shape=jax.ShapeDtypeStruct((2 * rows, tokens), jnp.float32),
        in_specs=specs,
        out_specs=pl.BlockSpec((depth, tokens), lambda i: (i, 0)),
        scratch_shapes=[
            pltpu.VMEM((min(SLOTS, steps + 1), depth, width), mine.dtype),
            pltpu.SemaphoreType.DMA((min(SLOTS, steps + 1),)),
        ],
        cost_estimate=pl.CostEstimate(
            flops=4 * rows * width * tokens,
            bytes_accessed=4 * rows * width + 2 * tokens * width + 8 * rows * tokens,
            transcendentals=0,
        ),
    )(*operands)


def rows_of(stack, rows):
    flat = jnp.concatenate(stack, axis=0)
    return jnp.pad(flat, ((0, rows - flat.shape[0]), (0, 0)))


def compute(hidden, head_weight, ref_logits, token_ids, end_pos, loss_mask, scores):
    batch, segment, width = hidden.shape
    rows, vocab_dev = head_weight.shape
    seq_size = lax.axis_size("seq")
    vocab_size = lax.axis_size("vocab")
    chips = seq_size // CORES
    seq = lax.axis_index("seq")
    vocab = lax.axis_index("vocab")
    chip, core = seq // CORES, seq % CORES
    vocab_start = vocab * vocab_dev

    def sibling(x):
        return lax.ppermute(x, "seq", [(s, s ^ 1) for s in range(seq_size)])

    def shift(x, by):
        pairs = [(s, (s + CORES * by) % seq_size) for s in range(seq_size)]
        return lax.ppermute(x, "seq", pairs)

    def features(owner):
        mine = lax.dynamic_slice_in_dim(hidden, owner * rows, rows, axis=2)
        other = lax.dynamic_slice_in_dim(hidden, (owner ^ 1) * rows, rows, axis=2)
        return jnp.concatenate([mine, other], axis=2)

    lead = LANES * max(1, vocab_dev // LANES * 2 // 25)
    chunks = [(0, lead)]
    chunks += [(lo + lead, hi + lead) for lo, hi in pieces(vocab_dev - lead, FORWARD_CHUNKS - 1)]
    outgoing = [features((seq - CORES * r) % seq_size) for r in range(1, chips)]
    own_states = features(seq)
    arriving = [shift(x, -r) for r, x in enumerate(outgoing, 1)]
    other_lead = sibling(lax.optimization_barrier((head_weight[:, :lead], *outgoing))[0])
    swapped = lax.optimization_barrier((head_weight, other_lead))[0]
    other_weight = sibling(swapped)
    weights = [(head_weight[:, lo:hi], other_weight[:, lo:hi]) for lo, hi in chunks]
    weights[0] = (head_weight[:, :lead], other_lead)

    def project(x, pair):
        mine, other = pair
        dot = functools.partial(
            jnp.einsum, "nbsd,dv->nbsv", preferred_element_type=jnp.float32
        )
        return dot(x[..., :rows], mine) + dot(x[..., rows:], other)

    def encode(x):
        top = jnp.maximum(jnp.max(jnp.abs(x), axis=-1), 1e-30)
        code = jnp.round(x * (LEVELS / top)[..., None]).astype(jnp.int16)
        return code, top / LEVELS

    def decode(code, step):
        return code.astype(jnp.float32) * step[..., None]

    states = jnp.stack([*arriving, own_states])
    logits, tops, totals, weighteds = [], [], [], []
    partials, sent = [], []
    for pair in weights:
        part = project(states, pair)
        partials.append(part[chips - 1])
        hops = []
        for r in range(1, chips):
            code, step = encode(part[r - 1])
            hops.append((shift(code, r), shift(step, r)))
        sent.append(hops)
    for j, (lo, hi) in enumerate(chunks):
        part = partials[j]
        for code, step in sent[j]:
            part = part + decode(code, step)
        logits.append(part)
        top = jnp.max(part, axis=2)
        expo = jnp.exp(part - top[:, :, None])
        refs = ref_logits[:, :, lo:hi].astype(jnp.float32)
        tops.append(top)
        totals.append(jnp.sum(expo, axis=2))
        weighteds.append(jnp.sum(expo * (part - refs), axis=2))
    refs = ref_logits.astype(jnp.float32)
    local_rtop = jnp.max(refs, axis=2)
    local_rtotal = jnp.sum(jnp.exp(refs - local_rtop[:, :, None]), axis=2)
    early = []
    for part in logits[:EARLY_CHUNKS]:
        code, step = encode(lax.optimization_barrier((part, sent[-2]))[0])
        early.append([(shift(code, -r), shift(step, -r)) for r in range(1, chips)])

    def merge(top_list, sums_list):
        top = functools.reduce(jnp.maximum, top_list)
        scales = [jnp.exp(t - top) for t in top_list]
        return top, [
            functools.reduce(jnp.add, [s * x for s, x in zip(scales, sums)])
            for sums in sums_list
        ]

    local_top, (local_total, local_weighted) = merge(tops, (totals, weighteds))
    stats = exchange(
        rows_of((local_top, local_total, local_weighted, local_rtop, local_rtotal), 16),
        "vocab",
        0,
    )
    stats = [
        [stats[d, batch * i : batch * (i + 1)] for d in range(vocab_size)] for i in range(5)
    ]
    top_policy, (total, weighted) = merge(stats[0], (stats[1], stats[2]))
    top_ref, (ref_total,) = merge(stats[3], (stats[4],))
    lse_policy = top_policy + jnp.log(total)
    lse_ref = top_ref + jnp.log(ref_total)
    kl_value = weighted / total - lse_policy + lse_ref
    position = seq * segment + lax.broadcasted_iota(jnp.int32, (1, segment), 1)
    live = ((loss_mask == 1) & (position <= end_pos[:, None])).astype(jnp.float32)
    at_end = (position == end_pos[:, None]).astype(jnp.float32)
    reward = -0.01 * kl_value * live + scores[:, None] * at_end
    table = rows_of((reward, live, lse_policy, token_ids.astype(jnp.float32)), 4 * batch)
    everyone = exchange(table, "seq", 1)
    all_reward, all_live, all_lse, all_tokens = [
        everyone[:, batch * i : batch * (i + 1)] for i in range(4)
    ]
    upper = (
        lax.broadcasted_iota(jnp.int32, (segment, segment), 0)
        >= lax.broadcasted_iota(jnp.int32, (segment, segment), 1)
    ).astype(jnp.float32)
    returns = jnp.einsum("nbs,st->nbt", all_reward, upper, precision=lax.Precision.HIGHEST)
    block_totals = jnp.sum(all_reward, axis=2)
    carried = [jnp.zeros_like(block_totals[0])]
    for s in range(seq_size - 1, 0, -1):
        carried.append(carried[-1] + block_totals[s])
    returns = returns + jnp.stack(carried[::-1])[:, :, None]
    count = jnp.maximum(jnp.sum(all_live), 1.0)
    mean = jnp.sum(all_live * returns) / count
    var = jnp.sum(all_live * returns * returns) / count - mean * mean
    all_advantages = (returns - mean) / jnp.sqrt(var + 1e-05)
    all_factor = all_live * all_advantages / count

    def of(x, owner):
        return lax.dynamic_index_in_dim(x, owner, 0, keepdims=False)

    def gradient(part, lo, hi, owner, tokens, lse):
        prob = jnp.exp(part - lse[:, :, None])
        column = vocab_start + lo + lax.broadcasted_iota(jnp.int32, (1, 1, hi - lo), 2)
        onehot = (column == tokens[:, :, None]).astype(jnp.float32)
        return (of(all_factor, owner)[:, :, None] * (prob - onehot)).astype(jnp.bfloat16)

    advantages = of(all_advantages, seq)
    grads = [
        gradient(part, lo, hi, seq, token_ids, lse_policy)
        for (lo, hi), part in zip(chunks, logits)
    ]
    logit_grad = jnp.concatenate(grads, axis=2)

    blocks = vocab_size // chips
    block = width // vocab_size
    part_rows = block // chips

    low_bits = [1 << i for i in range((vocab_size // CORES).bit_length() - 1)]
    top_bit = vocab_size // CORES

    def reduce_vocab(rest, turn):
        tokens = rest.shape[1]
        bits = low_bits[turn:] + low_bits[:turn]
        lengths = [2] * (len(low_bits) + 1)
        rest = rest.reshape(*lengths, part_rows, tokens)
        left = [top_bit] + low_bits[::-1]
        for bit in bits + [top_bit]:
            axis = left.index(bit)
            left.remove(bit)
            mine = (vocab // bit) % 2
            if bit == top_bit:
                mine = mine ^ core
            keep = lax.dynamic_index_in_dim(rest, mine, axis, keepdims=False)
            give = lax.dynamic_index_in_dim(rest, 1 - mine, axis, keepdims=False)
            rest = keep + lax.ppermute(
                give, "vocab", [(v, v ^ bit) for v in range(vocab_size)]
            )
        return rest

    def reduce_all(terms):
        return [
            reduce_vocab(terms[:, b * segment : (b + 1) * segment], b % 2)
            for b in range(batch)
        ]

    flat = [x.reshape(batch * segment, -1) for x in grads]
    late = [[shift(g, -r) for r in range(1, chips)] for g in flat[EARLY_CHUNKS:]]
    received = []
    for r in range(1, chips):
        owner = (seq + CORES * r) % seq_size
        tokens = of(all_tokens, owner).astype(jnp.int32)
        lse = of(all_lse, owner)
        first = [
            gradient(decode(*hops[r - 1]), lo, hi, owner, tokens, lse).reshape(batch * segment, -1)
            for (lo, hi), hops in zip(chunks, early)
        ]
        received.append(first + [hops[r - 1] for hops in late])

    latest = back(head_weight, other_weight, 0, lax.optimization_barrier(flat))
    owned = [reduce_all(latest)]
    for arrived in received:
        total = None
        turn = len(chunks) - LAST_CHUNKS
        for first, last in ((0, turn), (turn, len(chunks))):
            group = lax.optimization_barrier((latest, *arrived[first:last]))[1:]
            total = back(head_weight, other_weight, chunks[first][0], group, total)
            latest = total
        owned.append(reduce_all(total))
    held = jnp.stack([jnp.stack(parts, axis=1) for parts in owned]).astype(jnp.bfloat16)

    mine_q = vocab % chips
    source = vocab // blocks
    hidden_grad = jnp.zeros((chips, part_rows, batch, segment), jnp.bfloat16)
    for k in range(chips):
        pairs = []
        for s in range(seq_size):
            for v in range(vocab_size):
                y, c = divmod(s, CORES)
                to = ((y + k - v % chips) % chips) * CORES + c
                pairs.append((s * vocab_size + v, to * vocab_size + blocks * y + v // chips))
        out = lax.dynamic_index_in_dim(held, (k - mine_q) % chips, 0, keepdims=False)
        got = lax.ppermute(out, ("seq", "vocab"), pairs)
        hidden_grad = lax.dynamic_update_index_in_dim(
            hidden_grad, got, (k - (chip - source)) % chips, 0
        )
    hidden_grad = jnp.transpose(hidden_grad.reshape(block, batch, segment), (1, 2, 0))
    return (logit_grad, hidden_grad, advantages)


def solution(mesh):
    in_specs = (
        P(None, "seq", None),
        P("seq", "vocab"),
        P(None, "seq", "vocab"),
        P(None, "seq"),
        P(),
        P(None, "seq"),
        P(),
    )
    out_specs = (P(None, "seq", "vocab"), P(None, "seq", "vocab"), P(None, "seq"))
    return jax.shard_map(
        compute, mesh=mesh, in_specs=in_specs, out_specs=out_specs, check_vma=False
    )
```

```python
import functools

import jax
import jax.numpy as jnp
from jax import lax
from jax.experimental import pallas as pl
from jax.experimental.pallas import tpu as pltpu
from jax.sharding import PartitionSpec as P


CORES = 2
FORWARD_CHUNKS = 8
EARLY_CHUNKS = 3
LAST_CHUNKS = 2
LANES = 128
RING = 256 * 9728
SLOTS = 3
LEVELS = 32767.0


def pieces(extent, parts, unit=128):
    blocks = extent // unit
    edges = [unit * (blocks * i // parts) for i in range(parts)] + [extent]
    return [(lo, hi) for lo, hi in zip(edges[:-1], edges[1:]) if hi > lo]


def exchange_kernel(axis, n, x_ref, out_ref, send_sem, recv_sem, local_sem):
    me = lax.axis_index(axis)
    barrier = pltpu.get_barrier_semaphore()
    for k in range(1, n):
        pl.semaphore_signal(
            barrier,
            inc=1,
            device_id={axis: lax.rem(me + k, n)},
            device_id_type=pl.DeviceIdType.MESH,
        )
    own = pltpu.make_async_copy(x_ref, out_ref.at[me], local_sem)
    own.start()
    pl.semaphore_wait(barrier, n - 1)
    copies = []
    for k in range(1, n):
        copy = pltpu.make_async_remote_copy(
            src_ref=x_ref,
            dst_ref=out_ref.at[me],
            send_sem=send_sem.at[k],
            recv_sem=recv_sem.at[k],
            device_id={axis: lax.rem(me + k, n)},
            device_id_type=pl.DeviceIdType.MESH,
        )
        copy.start()
        copies.append(copy)
    own.wait()
    for copy in copies:
        copy.wait()


def exchange(x, axis, collective_id):
    n = lax.axis_size(axis)
    return pl.pallas_call(
        functools.partial(exchange_kernel, axis, n),
        out_shape=jax.ShapeDtypeStruct((n,) + x.shape, x.dtype),
        in_specs=[pl.BlockSpec(memory_space=pltpu.VMEM)],
        out_specs=pl.BlockSpec(memory_space=pltpu.VMEM),
        scratch_shapes=[
            pltpu.SemaphoreType.DMA((n,)),
            pltpu.SemaphoreType.DMA((n,)),
            pltpu.SemaphoreType.DMA,
        ],
        compiler_params=pltpu.CompilerParams(
            collective_id=collective_id, has_side_effects=True
        ),
    )(x)


def back_kernel(steps, depth, lo, widths, has_base, *refs):
    mine_ref, other_ref = refs[:2]
    grads = refs[2 : 2 + len(widths)]
    base = refs[2 + len(widths)] if has_base else None
    out_ref, ring, sems = refs[-3:]
    slots = ring.shape[0]
    step = pl.program_id(0)

    def copy(w_ref, row, slot):
        rows = pl.ds(pl.multiple_of(row * depth, depth), depth)
        return pltpu.make_async_copy(
            w_ref.at[rows, lo : lo + sum(widths)], ring.at[slot], sems.at[slot]
        )

    def fetch(item):
        slot = lax.rem(item, slots)
        pl.when(item < steps)(lambda: copy(mine_ref, item, slot).start())
        pl.when((item >= steps) & (item < 2 * steps))(
            lambda: copy(other_ref, item - steps, slot).start()
        )

    @pl.when(step == 0)
    def _():
        for item in range(slots - 1):
            fetch(jnp.int32(item))

    fetch(step + slots - 1)
    slot = lax.rem(step, slots)
    copy(mine_ref, 0, slot).wait()
    total = None
    start = 0
    for grad, width in zip(grads, widths):
        term = lax.dot_general(
            ring[slot, :, start : start + width],
            grad[...],
            (((1,), (1,)), ((), ())),
            preferred_element_type=jnp.float32,
        )
        total = term if total is None else total + term
        start += width
    out_ref[...] = total if base is None else total + base[...]


def back(mine, other, lo, grads, base=None):
    rows = mine.shape[0]
    tokens = grads[0].shape[0]
    widths = [g.shape[1] for g in grads]
    width = sum(widths)
    fits = [rows // n for n in range(1, rows // 16 + 1) if rows % (16 * n) == 0]
    depth = next((d for d in fits if d * width <= RING), 16)
    steps = rows // depth
    specs = [pl.BlockSpec(memory_space=pl.ANY)] * 2
    specs += [
        pl.BlockSpec((tokens, w), lambda i: (0, 0), pipeline_mode=pl.Buffered(1)) for w in widths
    ]
    operands = [mine, other, *grads]
    if base is not None:
        specs.append(pl.BlockSpec((depth, tokens), lambda i: (i, 0)))
        operands.append(base)
    return pl.pallas_call(
        functools.partial(back_kernel, steps, depth, lo, widths, base is not None),
        grid=(2 * steps,),
        out_shape=jax.ShapeDtypeStruct((2 * rows, tokens), jnp.float32),
        in_specs=specs,
        out_specs=pl.BlockSpec((depth, tokens), lambda i: (i, 0)),
        scratch_shapes=[
            pltpu.VMEM((min(SLOTS, steps + 1), depth, width), mine.dtype),
            pltpu.SemaphoreType.DMA((min(SLOTS, steps + 1),)),
        ],
        cost_estimate=pl.CostEstimate(
            flops=4 * rows * width * tokens,
            bytes_accessed=4 * rows * width + 2 * tokens * width + 8 * rows * tokens,
            transcendentals=0,
        ),
    )(*operands)


def fold_kernel(orders, top_bit, h_ref, out_ref, *scratch):
    stages = len(orders[0])
    batch = len(orders)
    segment = out_ref.shape[2]
    codes = scratch[: batch * stages]
    landed = scratch[batch * stages : 2 * batch * stages]
    sums = scratch[2 * batch * stages : 3 * batch * stages]
    steps_out, steps_in, send_sem, recv_sem = scratch[3 * batch * stages :]
    v = lax.axis_index("vocab")
    core = lax.rem(lax.axis_index("seq"), CORES)

    def side(bit):
        return lax.rem(v // bit, 2)

    def partner(bit):
        return {"vocab": v + bit * (1 - 2 * side(bit))}

    barrier = pltpu.get_barrier_semaphore()
    for bit in orders[0]:
        pl.semaphore_signal(
            barrier, inc=1, device_id=partner(bit), device_id_type=pl.DeviceIdType.MESH
        )
    pl.semaphore_wait(barrier, stages)

    left = [[top_bit] + sorted((x for x in o if x != top_bit), reverse=True) for o in orders]
    flights = {}

    def load(b, stage, block):
        if stage == 0:
            return h_ref[block, :, b * segment : (b + 1) * segment]
        return sums[b * stages + stage - 1][block]

    def place(b, stage, item, kept):
        bit = orders[b][stage]
        axis = left[b].index(bit)
        stride = 2 ** (len(left[b]) - 1 - axis)
        mine = side(bit)
        if bit == top_bit:
            mine = lax.rem(mine + core, 2)
        chosen = mine if kept else 1 - mine
        return (item // stride * 2 + chosen) * stride + lax.rem(item, stride)

    def send(b, stage):
        slot = b * stages + stage
        count = codes[slot].shape[0]

        def widest(item, top):
            x = load(b, stage, place(b, stage, item, False))
            return jnp.maximum(top, jnp.max(jnp.abs(x), axis=0, keepdims=True))

        top = lax.fori_loop(0, count, widest, jnp.full((1, segment), 1e-30, jnp.float32))
        steps_out[slot] = jnp.broadcast_to(top / LEVELS, steps_out.shape[1:])

        def encode(item, carry):
            x = load(b, stage, place(b, stage, item, False))
            code = jnp.round(x * (LEVELS / top)).astype(jnp.int32)
            codes[slot][item] = code.astype(jnp.int16)
            return carry

        lax.fori_loop(0, count, encode, 0)
        flights[b, stage] = []
        for part, (src, dst) in enumerate(
            ((codes[slot], landed[slot]), (steps_out.at[slot], steps_in.at[slot]))
        ):
            copy = pltpu.make_async_remote_copy(
                src_ref=src,
                dst_ref=dst,
                send_sem=send_sem.at[slot, part],
                recv_sem=recv_sem.at[slot, part],
                device_id=partner(orders[b][stage]),
                device_id_type=pl.DeviceIdType.MESH,
            )
            copy.start()
            flights[b, stage].append(copy)

    def add(b, stage):
        slot = b * stages + stage
        for copy in flights[b, stage]:
            copy.wait()
        step = steps_in[slot][:1]

        def body(item, carry):
            kept = load(b, stage, place(b, stage, item, True))
            other = landed[slot][item].astype(jnp.int32).astype(jnp.float32)
            sums[slot][item] = kept + other * step
            return carry

        lax.fori_loop(0, codes[slot].shape[0], body, 0)
        left[b].remove(orders[b][stage])

    for b in range(batch):
        send(b, 0)
    for stage in range(stages):
        for b in range(batch):
            add(b, stage)
            if stage + 1 < stages:
                send(b, stage + 1)
            else:
                out_ref[b] = sums[b * stages + stage][0].astype(jnp.bfloat16)


def fold(terms, orders, top_bit, segment, collective_id):
    stages = len(orders[0])
    part_rows = terms.shape[0] >> stages
    counts = [2 ** (stages - 1 - i) for _ in orders for i in range(stages)]
    arrays = [
        pltpu.VMEM((n, part_rows, segment), kind)
        for kind in (jnp.int16, jnp.int16, jnp.float32)
        for n in counts
    ]
    return pl.pallas_call(
        functools.partial(fold_kernel, orders, top_bit),
        out_shape=jax.ShapeDtypeStruct((len(orders), part_rows, segment), jnp.bfloat16),
        in_specs=[pl.BlockSpec(memory_space=pltpu.VMEM)],
        out_specs=pl.BlockSpec(memory_space=pltpu.VMEM),
        scratch_shapes=[
            *arrays,
            pltpu.VMEM((len(counts), 8, segment), jnp.float32),
            pltpu.VMEM((len(counts), 8, segment), jnp.float32),
            pltpu.SemaphoreType.DMA((len(counts), 2)),
            pltpu.SemaphoreType.DMA((len(counts), 2)),
        ],
        compiler_params=pltpu.CompilerParams(
            collective_id=collective_id, has_side_effects=True
        ),
    )(terms.reshape(2**stages, part_rows, terms.shape[1]))


def rows_of(stack, rows):
    flat = jnp.concatenate(stack, axis=0)
    return jnp.pad(flat, ((0, rows - flat.shape[0]), (0, 0)))


def compute(hidden, head_weight, ref_logits, token_ids, end_pos, loss_mask, scores):
    batch, segment, width = hidden.shape
    rows, vocab_dev = head_weight.shape
    seq_size = lax.axis_size("seq")
    vocab_size = lax.axis_size("vocab")
    chips = seq_size // CORES
    seq = lax.axis_index("seq")
    vocab = lax.axis_index("vocab")
    chip = seq // CORES
    vocab_start = vocab * vocab_dev

    def sibling(x):
        return lax.ppermute(x, "seq", [(s, s ^ 1) for s in range(seq_size)])

    def shift(x, by):
        pairs = [(s, (s + CORES * by) % seq_size) for s in range(seq_size)]
        return lax.ppermute(x, "seq", pairs)

    def features(owner):
        mine = lax.dynamic_slice_in_dim(hidden, owner * rows, rows, axis=2)
        other = lax.dynamic_slice_in_dim(hidden, (owner ^ 1) * rows, rows, axis=2)
        return jnp.concatenate([mine, other], axis=2)

    lead = LANES * max(1, vocab_dev // LANES * 2 // 25)
    chunks = [(0, lead)]
    chunks += [(lo + lead, hi + lead) for lo, hi in pieces(vocab_dev - lead, FORWARD_CHUNKS - 1)]
    outgoing = [features((seq - CORES * r) % seq_size) for r in range(1, chips)]
    own_states = features(seq)
    arriving = [shift(x, -r) for r, x in enumerate(outgoing, 1)]
    other_lead = sibling(lax.optimization_barrier((head_weight[:, :lead], *outgoing))[0])
    swapped = lax.optimization_barrier((head_weight, other_lead))[0]
    other_weight = sibling(swapped)
    weights = [(head_weight[:, lo:hi], other_weight[:, lo:hi]) for lo, hi in chunks]
    weights[0] = (head_weight[:, :lead], other_lead)

    def project(x, pair):
        mine, other = pair
        dot = functools.partial(
            jnp.einsum, "nbsd,dv->nbsv", preferred_element_type=jnp.float32
        )
        return dot(x[..., :rows], mine) + dot(x[..., rows:], other)

    def encode(x):
        top = jnp.maximum(jnp.max(jnp.abs(x), axis=-1), 1e-30)
        code = jnp.round(x * (LEVELS / top)[..., None]).astype(jnp.int16)
        return code, top / LEVELS

    def decode(code, step):
        return code.astype(jnp.float32) * step[..., None]

    states = jnp.stack([*arriving, own_states])
    logits, tops, totals, weighteds = [], [], [], []
    partials, sent = [], []
    for pair in weights:
        part = project(states, pair)
        partials.append(part[chips - 1])
        hops = []
        for r in range(1, chips):
            code, step = encode(part[r - 1])
            hops.append((shift(code, r), shift(step, r)))
        sent.append(hops)
    for j, (lo, hi) in enumerate(chunks):
        part = partials[j]
        for code, step in sent[j]:
            part = part + decode(code, step)
        logits.append(part)
        top = jnp.max(part, axis=2)
        expo = jnp.exp(part - top[:, :, None])
        refs = ref_logits[:, :, lo:hi].astype(jnp.float32)
        tops.append(top)
        totals.append(jnp.sum(expo, axis=2))
        weighteds.append(jnp.sum(expo * (part - refs), axis=2))
    refs = ref_logits.astype(jnp.float32)
    local_rtop = jnp.max(refs, axis=2)
    local_rtotal = jnp.sum(jnp.exp(refs - local_rtop[:, :, None]), axis=2)
    early = []
    for part in logits[:EARLY_CHUNKS]:
        code, step = encode(lax.optimization_barrier((part, sent[-2]))[0])
        early.append([(shift(code, -r), shift(step, -r)) for r in range(1, chips)])

    def merge(top_list, sums_list):
        top = functools.reduce(jnp.maximum, top_list)
        scales = [jnp.exp(t - top) for t in top_list]
        return top, [
            functools.reduce(jnp.add, [s * x for s, x in zip(scales, sums)])
            for sums in sums_list
        ]

    local_top, (local_total, local_weighted) = merge(tops, (totals, weighteds))
    stats = exchange(
        rows_of((local_top, local_total, local_weighted, local_rtop, local_rtotal), 16),
        "vocab",
        0,
    )
    stats = [
        [stats[d, batch * i : batch * (i + 1)] for d in range(vocab_size)] for i in range(5)
    ]
    top_policy, (total, weighted) = merge(stats[0], (stats[1], stats[2]))
    top_ref, (ref_total,) = merge(stats[3], (stats[4],))
    lse_policy = top_policy + jnp.log(total)
    lse_ref = top_ref + jnp.log(ref_total)
    kl_value = weighted / total - lse_policy + lse_ref
    position = seq * segment + lax.broadcasted_iota(jnp.int32, (1, segment), 1)
    live = ((loss_mask == 1) & (position <= end_pos[:, None])).astype(jnp.float32)
    at_end = (position == end_pos[:, None]).astype(jnp.float32)
    reward = -0.01 * kl_value * live + scores[:, None] * at_end
    table = rows_of((reward, live, lse_policy, token_ids.astype(jnp.float32)), 4 * batch)
    everyone = exchange(table, "seq", 1)
    all_reward, all_live, all_lse, all_tokens = [
        everyone[:, batch * i : batch * (i + 1)] for i in range(4)
    ]
    upper = (
        lax.broadcasted_iota(jnp.int32, (segment, segment), 0)
        >= lax.broadcasted_iota(jnp.int32, (segment, segment), 1)
    ).astype(jnp.float32)
    returns = jnp.einsum("nbs,st->nbt", all_reward, upper, precision=lax.Precision.HIGHEST)
    block_totals = jnp.sum(all_reward, axis=2)
    carried = [jnp.zeros_like(block_totals[0])]
    for s in range(seq_size - 1, 0, -1):
        carried.append(carried[-1] + block_totals[s])
    returns = returns + jnp.stack(carried[::-1])[:, :, None]
    count = jnp.maximum(jnp.sum(all_live), 1.0)
    mean = jnp.sum(all_live * returns) / count
    var = jnp.sum(all_live * returns * returns) / count - mean * mean
    all_advantages = (returns - mean) / jnp.sqrt(var + 1e-05)
    all_factor = all_live * all_advantages / count

    def of(x, owner):
        return lax.dynamic_index_in_dim(x, owner, 0, keepdims=False)

    def gradient(part, lo, hi, owner, tokens, lse):
        prob = jnp.exp(part - lse[:, :, None])
        column = vocab_start + lo + lax.broadcasted_iota(jnp.int32, (1, 1, hi - lo), 2)
        onehot = (column == tokens[:, :, None]).astype(jnp.float32)
        return (of(all_factor, owner)[:, :, None] * (prob - onehot)).astype(jnp.bfloat16)

    advantages = of(all_advantages, seq)
    grads = [
        gradient(part, lo, hi, seq, token_ids, lse_policy)
        for (lo, hi), part in zip(chunks, logits)
    ]
    logit_grad = jnp.concatenate(grads, axis=2)

    blocks = vocab_size // chips
    block = width // vocab_size
    part_rows = block // chips

    low_bits = [1 << i for i in range((vocab_size // CORES).bit_length() - 1)]
    top_bit = vocab_size // CORES

    orders = []
    for b in range(batch):
        turn = b % 2
        orders.append(low_bits[turn:] + low_bits[:turn] + [top_bit])

    def reduce_all(terms, r):
        return fold(terms, orders, top_bit, segment, 2 + r)

    flat = [x.reshape(batch * segment, -1) for x in grads]
    late = [[shift(g, -r) for r in range(1, chips)] for g in flat[EARLY_CHUNKS:]]
    received = []
    for r in range(1, chips):
        owner = (seq + CORES * r) % seq_size
        tokens = of(all_tokens, owner).astype(jnp.int32)
        lse = of(all_lse, owner)
        first = [
            gradient(decode(*hops[r - 1]), lo, hi, owner, tokens, lse).reshape(batch * segment, -1)
            for (lo, hi), hops in zip(chunks, early)
        ]
        received.append(first + [hops[r - 1] for hops in late])

    latest = back(head_weight, other_weight, 0, lax.optimization_barrier(flat))
    owned = [reduce_all(latest, 0)]
    for r, arrived in enumerate(received, 1):
        total = None
        turn = len(chunks) - LAST_CHUNKS
        for first, last in ((0, turn), (turn, len(chunks))):
            group = lax.optimization_barrier((latest, *arrived[first:last]))[1:]
            total = back(head_weight, other_weight, chunks[first][0], group, total)
            latest = total
        owned.append(reduce_all(total, r))
    held = jnp.stack(owned)

    mine_q = vocab % chips
    source = vocab // blocks
    hidden_grad = jnp.zeros((chips, batch, part_rows, segment), jnp.bfloat16)
    for k in range(chips):
        pairs = []
        for s in range(seq_size):
            for v in range(vocab_size):
                y, c = divmod(s, CORES)
                to = ((y + k - v % chips) % chips) * CORES + c
                pairs.append((s * vocab_size + v, to * vocab_size + blocks * y + v // chips))
        out = lax.dynamic_index_in_dim(held, (k - mine_q) % chips, 0, keepdims=False)
        got = lax.ppermute(out, ("seq", "vocab"), pairs)
        hidden_grad = lax.dynamic_update_index_in_dim(
            hidden_grad, got, (k - (chip - source)) % chips, 0
        )
    hidden_grad = jnp.transpose(hidden_grad, (1, 3, 0, 2)).reshape(batch, segment, block)
    return (logit_grad, hidden_grad, advantages)


def solution(mesh):
    in_specs = (
        P(None, "seq", None),
        P("seq", "vocab"),
        P(None, "seq", "vocab"),
        P(None, "seq"),
        P(),
        P(None, "seq"),
        P(),
    )
    out_specs = (P(None, "seq", "vocab"), P(None, "seq", "vocab"), P(None, "seq"))
    return jax.shard_map(
        compute, mesh=mesh, in_specs=in_specs, out_specs=out_specs, check_vma=False
    )
```
